32 devices in a mesh: section: 4 (over z), th: 4 (over y, x), tw: 2 (over core).
Axes of the slice: x: 2, y: 2, z: 4, core: 2. Of those that a mesh axis runs over, the one named last changes fastest.
Arguments:
- features: bfloat16 [16, 64, 64, 128], P('section', 'th', 'tw'), may hold values from -11 to 11, as said below
- norm_gain: float32 [128], replicated, may hold values from 0.25 to 1.75
- norm_shift: float32 [128], replicated, may hold values from -3 to 3
- first_kernel: bfloat16 [3, 3, 3, 128, 128], replicated, may hold values from -0.109375 to 0.109375
- second_gain: float32 [128], replicated, may hold values from 0.25 to 1.75
- second_shift: float32 [128], replicated, may hold values from -3 to 3
- second_kernel: bfloat16 [3, 3, 3, 128, 128], replicated, may hold values from -0.109375 to 0.109375
Outputs:
- block_out: bfloat16 [16, 64, 64, 128], P('section', 'th', 'tw')
The draws below stay inside these ranges and needn't reach their ends.
Inputs may be any that keep to these rules, and one draw needn't show every extreme that they name: `features`: activations of order one.
All inputs are finite; a program needn't handle non-finite values.
Results may differ from the reference program's by a relative error of at most 0.0038.
Values may be sent and summed in bfloat16 or wider, within the bound.
A program may use at most 128 MiB of HBM per device.

```python
import jax
import jax.numpy as jnp
from jax import lax

C = 128
GROUPS = 32
FRAMES = 16
HEIGHT = 64
WIDTH = 64


def draw_features(key, part):
    base = jax.random.fold_in(key, 7319)
    key_offset = jax.random.fold_in(base, 0)
    key_noise = jax.random.fold_in(base, 2)
    key_frame = jax.random.fold_in(base, 3)
    key_scale = jax.random.fold_in(base, 4)
    key_row = jax.random.fold_in(base, 5)
    key_col = jax.random.fold_in(base, 6)
    time_frac = jnp.arange(FRAMES, dtype=jnp.float32) / max(FRAMES - 1, 1)
    shape = (FRAMES, HEIGHT, WIDTH, C)
    offset = 0.7 * jax.random.normal(key_offset, (C,), jnp.float32)
    noise = jnp.clip(jax.random.normal(key_noise, shape, jnp.float32), -4.0, 4.0)
    frame_off = 1.0 - 2.0 * time_frac + jax.random.uniform(key_frame, (FRAMES,), jnp.float32, -0.5, 0.5)
    frame_scale = jax.random.uniform(key_scale, (FRAMES,), jnp.float32, 0.4, 1.6)
    row_off = jax.random.uniform(key_row, (HEIGHT,), jnp.float32, 0.4, 1.6)
    col_level = jax.random.uniform(key_col, (WIDTH,), jnp.float32, 0.6, 1.8)
    mean_part = offset[None, None, None, :] * frame_off[:, None, None, None] * row_off[None, :, None, None]
    noise_part = frame_scale[:, None, None, None] * col_level[None, None, :, None] * noise
    return jnp.clip(mean_part + noise_part, -11.0, 11.0).astype(jnp.bfloat16)


def normal_values(stream_key, shape, deviation, reach, kind=jnp.bfloat16):
    drawn = deviation * jax.random.normal(stream_key, shape, jnp.float32)
    return jnp.clip(drawn, min=-reach, max=reach).astype(kind)


def setup_inputs(seed: int = 0) -> dict:
    streams_of = jax.random.split(jax.random.key(seed), 8)
    return {
        "features": draw_features(jax.random.fold_in(streams_of[7], 71), 0),
        "norm_gain": jnp.clip(1.0 + 0.15 * jax.random.normal(streams_of[1], (C,), jnp.float32), 0.25, 1.75),
        "norm_shift": normal_values(streams_of[2], (C,), 0.5, 3.0, jnp.float32),
        "first_kernel": normal_values(streams_of[3], (3, 3, 3, C, C), (27 * C) ** -0.5, 0.109375),
        "second_gain": jnp.clip(1.0 + 0.15 * jax.random.normal(streams_of[4], (C,), jnp.float32), 0.25, 1.75),
        "second_shift": normal_values(streams_of[5], (C,), 0.5, 3.0, jnp.float32),
        "second_kernel": normal_values(streams_of[6], (3, 3, 3, C, C), (27 * C) ** -0.5, 0.109375),
    }


def causal_conv(padded, kernel):
    frames = padded.shape[0] - 2
    rows = padded.shape[1] - 2
    cols = padded.shape[2] - 2
    chans = padded.shape[3]
    stacked = jnp.concatenate([padded[:, :, d:d + cols, :] for d in range(3)], axis=-1)
    taps = kernel.reshape(3, 3, 3 * chans, kernel.shape[-1])
    total = jnp.zeros((frames * rows * cols, kernel.shape[-1]), jnp.float32)
    for dt in range(3):
        for dh in range(3):
            window = stacked[dt:dt + frames, dh:dh + rows].reshape(-1, 3 * chans)
            total = total + jnp.dot(window, taps[dt, dh], preferred_element_type=jnp.float32)
    return total.reshape(frames, rows, cols, kernel.shape[-1])

def group_norm_act(values, gain, shift):
    chans = values.shape[-1]
    grouped = values.astype(jnp.float32).reshape(-1, GROUPS, chans // GROUPS)
    mean = lax.optimization_barrier(jnp.mean(grouped, axis=(0, 2), keepdims=True))
    var = lax.optimization_barrier(jnp.mean((grouped - mean) ** 2, axis=(0, 2), keepdims=True))
    normed = ((grouped - mean) / jnp.sqrt(var + 1e-06)).reshape(values.shape) * gain + shift
    return jax.nn.silu(normed).astype(jnp.bfloat16)

def pad_clip(values):
    return jnp.pad(values, ((2, 0), (1, 1), (1, 1), (0, 0)))

def reference(features, norm_gain, norm_shift, first_kernel, second_gain, second_shift, second_kernel):
    first_act = group_norm_act(features, norm_gain, norm_shift)
    hidden = causal_conv(pad_clip(first_act), first_kernel)
    second_act = group_norm_act(hidden, second_gain, second_shift)
    branch = causal_conv(pad_clip(second_act), second_kernel)
    return (features.astype(jnp.float32) + branch).astype(jnp.bfloat16)
```

```python
import functools

import jax
import jax.numpy as jnp
from jax import lax
from jax.experimental import pallas as pl
from jax.experimental.pallas import tpu as pltpu
from jax.sharding import PartitionSpec as P

GROUPS = 32
LEAD = 8
AXES = ("section", "th", "tw")
SENDS = [(s, h, w) for s in (1, 0) for h in (0, -1, 1) for w in (0, -1, 1) if (s, h, w) != (0, 0, 0)]


def group_sum(row, per_group):
    lane = lax.broadcasted_iota(jnp.int32, row.shape, 1)
    chans = row.shape[1]
    step = 1
    while step < per_group:
        upper = lax.rem(lax.div(lane, step), 2) == 1
        row = row + jnp.where(upper, pltpu.roll(row, step, 1), pltpu.roll(row, chans - step, 1))
        step *= 2
    return row


def body(
    sizes, feat_hbm, gain1, shift1, k1_hbm, gain2, shift2, k2_hbm, out_hbm,
    feat, raw, result, hid, padded, cells, w1, w2, cols, frames_in, rows_in, cols_in, corners_in,
    mine, theirs, load_sem, out_sem, stat_send, stat_recv, halo_send, halo_recv,
):
    ns, nh, nw = sizes
    ndev = ns * nh * nw
    T, H, W, C = feat.shape
    PW = padded.shape[2]
    area = H * W
    flat = padded.reshape(padded.shape[0] * padded.shape[1] * PW, C)
    sec, th, tw = (lax.axis_index(a) for a in AXES)
    rank = (sec * nh + th) * nw + tw
    taps = k1_hbm.shape[0]
    third = taps // 3

    load = pltpu.make_async_copy(feat_hbm, feat, load_sem.at[0])
    load.start()
    weight_loads = []
    for n, (src, dst) in enumerate(((k1_hbm, w1), (k2_hbm, w2))):
        for half in range(2):
            weight_loads.append(
                pltpu.make_async_copy(
                    src,
                    dst.at[pl.ds(half * third, taps), pl.ds(half * C, C)],
                    load_sem.at[1 + 2 * n + half],
                )
            )

    def peer(d):
        other = lax.rem(rank + d, ndev)
        return (lax.div(other, nh * nw), lax.rem(lax.div(other, nw), nh), lax.rem(other, nw))

    barrier = pltpu.get_barrier_semaphore()

    def greet(d, c):
        pl.semaphore_signal(barrier, inc=1, device_id=peer(d), device_id_type=pl.DeviceIdType.MESH)
        return c

    lax.fori_loop(1, ndev, greet, 0)
    for w in weight_loads:
        w.start()
    for w in (w1, w2):
        w[3 * third : 4 * third, 0:C] = jnp.zeros((third, C), jnp.bfloat16)
        w[0:third, C : 2 * C] = jnp.zeros((third, C), jnp.bfloat16)

    def present(s, h, w):
        ok = True
        for v, at, count in ((s, sec, ns), (h, th, nh), (w, tw, nw)):
            if v < 0:
                ok = jnp.logical_and(ok, at > 0)
            if v > 0:
                ok = jnp.logical_and(ok, at < count - 1)
        return ok

    def halo_copy(n, k):
        s, h, w = SENDS[k]
        frames = pl.ds(T - 2, 2) if s else pl.ds(0, T)
        into = pl.ds(0, 2) if s else pl.ds(2, T)
        source = feat if n == 0 else raw
        hs, ws = (0 if h > 0 else 1), (0 if w > 0 else 1)
        if h == 0 and w == 0:
            src, dst = source.at[frames], frames_in.at[n]
        elif w == 0:
            src = source.at[frames, H - 1 if h > 0 else 0]
            dst = rows_in.at[n, hs, into]
        else:
            src = cols.at[n, 1 if w > 0 else 0, frames]
            dst = cols_in.at[n, ws, into] if h == 0 else corners_in.at[n, hs, ws, into]
        return pltpu.make_async_remote_copy(
            src_ref=src, dst_ref=dst,
            send_sem=halo_send.at[n, k], recv_sem=halo_recv.at[n, k],
            device_id=(sec + s, th + h, tw + w), device_id_type=pl.DeviceIdType.MESH,
        )

    def send_halo(n, which):
        for k, (s, h, w) in enumerate(SENDS):
            if s == which:
                @pl.when(present(s, h, w))
                def _():
                    halo_copy(n, k).start()

    def wait_halo(n, recv):
        for k, (s, h, w) in enumerate(SENDS):
            @pl.when(present(-s, -h, -w) if recv else present(s, h, w))
            def _():
                if recv:
                    halo_copy(n, k).wait_recv()
                else:
                    halo_copy(n, k).wait_send()

    def stat_copy(n, d):
        return pltpu.make_async_remote_copy(
            src_ref=mine.at[n], dst_ref=theirs.at[n, d - 1],
            send_sem=stat_send.at[n], recv_sem=stat_recv.at[n],
            device_id=peer(d), device_id_type=pl.DeviceIdType.MESH,
        )

    lane = lax.broadcasted_iota(jnp.int32, (1, C), 1)
    even = lax.rem(lane, 2) == 0

    def send_stats(n, total, squares):
        total = group_sum(jnp.sum(total, axis=0, keepdims=True), C // GROUPS)
        squares = group_sum(jnp.sum(squares, axis=0, keepdims=True), C // GROUPS)
        mine[n] = jnp.where(even, total, squares)

        def start(d, c):
            stat_copy(n, d).start()
            return c

        lax.fori_loop(1, ndev, start, 0)

    def all_stats(n, of):
        return pltpu.make_async_copy(theirs.at[n], theirs.at[n], of.at[n])

    def get_affine(n, gain, shift):
        all_stats(n, stat_recv).wait()
        both = jnp.sum(theirs[n], axis=0) + mine[n]
        total = jnp.where(even, both, pltpu.roll(both, 1, 1))
        squares = jnp.where(even, pltpu.roll(both, C - 1, 1), both)
        count = T * area * (C // GROUPS) * ndev
        mean = total / count
        var = squares / count - mean * mean
        scale = gain[...] / jnp.sqrt(var + 1e-06)
        return 0.5 * scale, 0.5 * (shift[...] - mean * scale)

    def fold(v):
        return jnp.sum(v.reshape(-1, 8, C), axis=0)

    load.wait()

    def first(t, carry):
        v = feat[t].astype(jnp.float32).reshape(area, C)
        hid[pl.ds(t * area, area), :] = v
        return carry[0] + fold(v), carry[1] + fold(v * v)

    zero = jnp.zeros((8, C), jnp.float32)
    sums = lax.fori_loop(0, T, first, (zero, zero))

    def take_cols(n):
        for side, j in ((0, 0), (1, W - 1)):
            edge = hid[pl.ds(j, T * H, stride=W), :]
            cols[n, side] = edge.astype(jnp.bfloat16).reshape(T, H, C)

    take_cols(0)
    pl.semaphore_wait(barrier, ndev - 1)
    send_stats(0, *sums)
    send_halo(0, 1)
    send_halo(0, 0)

    def activate(n, gain, shift):
        wait_halo(n, True)
        scale, bias = get_affine(n, gain, shift)

        def act(v):
            h = v * scale + bias
            return h * jnp.tanh(h) + h

        def inner(t, c):
            a = act(hid[pl.ds(t * area, area), :])
            padded[t + 2, 1 : H + 1, LEAD : LEAD + W] = a.reshape(H, W, C)
            return c

        lax.fori_loop(0, T, inner, 0)

        def before(t, c):
            a = act(frames_in[n, t].astype(jnp.float32).reshape(area, C))
            a = jnp.where(sec > 0, a, 0.0)
            padded[t, 1 : H + 1, LEAD : LEAD + W] = a.reshape(H, W, C)
            return c

        lax.fori_loop(0, 2, before, 0)

        def edges(t, c):
            known = jnp.logical_or(sec > 0, t >= 2)
            for hs, h in ((0, -1), (1, 1)):
                okh = jnp.logical_and(known, present(0, h, 0))
                i = 0 if hs == 0 else H + 1
                a = act(rows_in[n, hs, t].astype(jnp.float32))
                padded[t, i, LEAD : LEAD + W] = jnp.where(okh, a, 0.0)
                for ws, w in ((0, -1), (1, 1)):
                    okc = jnp.logical_and(okh, present(0, 0, w))
                    j = LEAD - 1 if ws == 0 else LEAD + W
                    a = act(corners_in[n, hs, ws, t].astype(jnp.float32))
                    a = a[H - 1 : H] if hs == 0 else a[0:1]
                    padded[t, i, j : j + 1] = jnp.where(okc, a, 0.0)
            for ws, w in ((0, -1), (1, 1)):
                okw = jnp.logical_and(known, present(0, 0, w))
                j = LEAD - 1 if ws == 0 else LEAD + W
                a = jnp.where(okw, act(cols_in[n, ws, t].astype(jnp.float32)), 0.0)
                flat[pl.ds((t * (H + 2) + 1) * PW + j, H, stride=PW), :] = a
            return c

        lax.fori_loop(0, T + 2, edges, 0)

        def shifted(t, c):
            for d in range(3):
                v = padded[t, :, LEAD - 1 + d : LEAD - 1 + d + W]
                cells[t, :, :, d * C : (d + 1) * C] = v.astype(jnp.bfloat16)
            return c

        lax.fori_loop(0, T + 2, shifted, 0)

    def conv(pair, w):
        parts = [
            cells[2 * pair + q, di : di + H].reshape(area, 3 * C)
            for q in range(4)
            for di in range(3)
        ]
        return jnp.dot(jnp.concatenate(parts, axis=-1), w[...], preferred_element_type=jnp.float32)

    activate(0, gain1, shift1)
    weight_loads[0].wait()
    weight_loads[1].wait()
    total = squares = zero
    for pair in reversed(range(T // 2)):
        both = conv(pair, w1)
        for f in range(2):
            v = both[:, f * C : (f + 1) * C]
            t = 2 * pair + f
            hid[t * area : (t + 1) * area, :] = v
            raw[t] = v.astype(jnp.bfloat16).reshape(H, W, C)
            total = total + fold(v)
            squares = squares + fold(v * v)
    take_cols(1)
    send_stats(1, total, squares)
    send_halo(1, 1)
    send_halo(1, 0)
    activate(1, gain2, shift2)
    weight_loads[2].wait()
    weight_loads[3].wait()
    stores = []
    for pair in range(T // 2):
        both = conv(pair, w2)
        for f in range(2):
            t = 2 * pair + f
            v = both[:, f * C : (f + 1) * C].reshape(H, W, C)
            result[t] = (feat[t].astype(jnp.float32) + v).astype(jnp.bfloat16)
        store = pltpu.make_async_copy(
            result.at[pl.ds(2 * pair, 2)], out_hbm.at[pl.ds(2 * pair, 2)], out_sem.at[pair]
        )
        store.start()
        stores.append(store)
    for n in range(2):
        wait_halo(n, False)
        all_stats(n, stat_send).wait()
    for store in stores:
        store.wait()


def shards(sizes, features, gain1, shift1, k1, gain2, shift2, k2):
    T, H, W, C = features.shape
    ndev = sizes[0] * sizes[1] * sizes[2]
    bf, f32 = jnp.bfloat16, jnp.float32
    any_spec = pl.BlockSpec(memory_space=pl.ANY)
    vmem = pl.BlockSpec(memory_space=pltpu.VMEM)
    flat = lambda k: k.reshape(-1, k.shape[-1])
    row = lambda v: v.reshape(1, C)
    return pl.pallas_call(
        functools.partial(body, sizes),
        out_shape=jax.ShapeDtypeStruct(features.shape, bf),
        in_specs=[any_spec, vmem, vmem, any_spec, vmem, vmem, any_spec],
        out_specs=any_spec,
        scratch_shapes=[
            pltpu.VMEM((T, H, W, C), bf),
            pltpu.VMEM((T, H, W, C), bf),
            pltpu.VMEM((T, H, W, C), bf),
            pltpu.VMEM((T * H * W, C), f32),
            pltpu.VMEM((T + 2, H + 2, W + 2 * LEAD, C), f32),
            pltpu.VMEM((T + 2, H + 2, W, 3 * C), bf),
            pltpu.VMEM((4 * 9 * C, 2 * C), bf),
            pltpu.VMEM((4 * 9 * C, 2 * C), bf),
            pltpu.VMEM((2, 2, T, H, C), bf),
            pltpu.VMEM((2, 2, H, W, C), bf),
            pltpu.VMEM((2, 2, T + 2, W, C), bf),
            pltpu.VMEM((2, 2, T + 2, H, C), bf),
            pltpu.VMEM((2, 2, 2, T + 2, H, C), bf),
            pltpu.VMEM((2, 1, C), f32),
            pltpu.VMEM((2, ndev - 1, 1, C), f32),
            pltpu.SemaphoreType.DMA((5,)),
            pltpu.SemaphoreType.DMA((T // 2,)),
            pltpu.SemaphoreType.DMA((2,)),
            pltpu.SemaphoreType.DMA((2,)),
            pltpu.SemaphoreType.DMA((2, len(SENDS))),
            pltpu.SemaphoreType.DMA((2, len(SENDS))),
        ],
        compiler_params=pltpu.CompilerParams(
            collective_id=0, has_side_effects=True, vmem_limit_bytes=60 << 20
        ),
    )(features, row(gain1), row(shift1), flat(k1), row(gain2), row(shift2), flat(k2))


def solution(mesh):
    sizes = tuple(mesh.shape[a] for a in AXES)
    placed = (P("section", "th", "tw", None), P(), P(), P(), P(), P(), P())
    return jax.shard_map(
        functools.partial(shards, sizes),
        mesh=mesh,
        in_specs=placed,
        out_specs=P("section", "th", "tw", None),
        check_vma=False,
    )
```

```python
import functools

import jax
import jax.numpy as jnp
from jax import lax
from jax.experimental import pallas as pl
from jax.experimental.pallas import tpu as pltpu
from jax.sharding import PartitionSpec as P

GROUPS = 32
LEAD = 8
AXES = ("section", "th", "tw")
NEAR = [(0, h, w, 0) for h in (0, -1, 1) for w in (0, -1, 1) if (h, w) != (0, 0)]
EARLY = [(1, 0, 0, 0)]
LATE = [(1, 0, 0, 1)] + [(1, h, w, 0) for h in (0, -1, 1) for w in (0, -1, 1) if (h, w) != (0, 0)]
SENDS = NEAR + EARLY + LATE


def group_sum(row, per_group):
    lane = lax.broadcasted_iota(jnp.int32, row.shape, 1)
    chans = row.shape[1]
    step = 1
    while step < per_group:
        upper = lax.rem(lax.div(lane, step), 2) == 1
        row = row + jnp.where(upper, pltpu.roll(row, step, 1), pltpu.roll(row, chans - step, 1))
        step *= 2
    return row


def body(
    sizes, feat_hbm, gain1, shift1, k1_hbm, gain2, shift2, k2_hbm, out_hbm,
    feat, raw, result, hid, padded, cells, acc, w1, w2, cols, corners, frames_in, rows_in, cols_in, corners_in,
    mine, theirs, load_sem, out_sem, stat_send, stat_recv, halo_send, halo_recv,
):
    ns, nh, nw = sizes
    ndev = ns * nh * nw
    T, H, W, C = feat.shape
    PW = padded.shape[2]
    area = H * W
    flat = padded.reshape(padded.shape[0] * padded.shape[1] * PW, C)
    sec, th, tw = (lax.axis_index(a) for a in AXES)
    rank = (sec * nh + th) * nw + tw
    taps = k1_hbm.shape[0]
    third = taps // 3

    load = pltpu.make_async_copy(feat_hbm, feat, load_sem.at[0])
    load.start()
    weight_loads = []
    for n, (src, dst) in enumerate(((k1_hbm, w1), (k2_hbm, w2))):
        for half in range(2):
            weight_loads.append(
                pltpu.make_async_copy(
                    src,
                    dst.at[pl.ds(half * third, taps), pl.ds(half * C, C)],
                    load_sem.at[1 + 2 * n + half],
                )
            )

    def peer(d):
        other = lax.rem(rank + d, ndev)
        return (lax.div(other, nh * nw), lax.rem(lax.div(other, nw), nh), lax.rem(other, nw))

    barrier = pltpu.get_barrier_semaphore()

    def greet(d, c):
        pl.semaphore_signal(barrier, inc=1, device_id=peer(d), device_id_type=pl.DeviceIdType.MESH)
        return c

    lax.fori_loop(1, ndev, greet, 0)
    for w in weight_loads:
        w.start()
    for w in (w1, w2):
        w[3 * third : 4 * third, 0:C] = jnp.zeros((third, C), jnp.bfloat16)
        w[0:third, C : 2 * C] = jnp.zeros((third, C), jnp.bfloat16)

    def present(s, h, w):
        ok = True
        for v, at, count in ((s, sec, ns), (h, th, nh), (w, tw, nw)):
            if v < 0:
                ok = jnp.logical_and(ok, at > 0)
            if v > 0:
                ok = jnp.logical_and(ok, at < count - 1)
        return ok

    chunk = H // 2

    def halo_copy(n, kind):
        s, h, w, part = kind
        k = SENDS.index(kind)
        frames = pl.ds(T - 2, 2) if s else pl.ds(0, T)
        into = pl.ds(0, 2) if s else pl.ds(2, T)
        source = feat if n == 0 else raw
        hs, ws = (0 if h > 0 else 1), (0 if w > 0 else 1)
        if h == 0 and w == 0:
            if part == 0:
                src, dst = source.at[T - 2, pl.ds(0, chunk)], frames_in.at[n, 0, pl.ds(0, chunk)]
            else:
                rest = pl.ds(chunk, 2 * H - chunk)
                src = source.at[pl.ds(T - 2, 2)].reshape(2 * H, W, C).at[rest]
                dst = frames_in.at[n].reshape(2 * H, W, C).at[rest]
        elif w == 0:
            src = source.at[frames, H - 1 if h > 0 else 0]
            dst = rows_in.at[n, hs, into]
        elif h == 0:
            src = cols.at[n, 1 if w > 0 else 0, frames]
            dst = cols_in.at[n, ws, into]
        else:
            src = corners.at[n, 1 if h > 0 else 0, 1 if w > 0 else 0, frames]
            dst = corners_in.at[n, hs, ws, into]
        return pltpu.make_async_remote_copy(
            src_ref=src, dst_ref=dst,
            send_sem=halo_send.at[n, k], recv_sem=halo_recv.at[n, k],
            device_id=(sec + s, th + h, tw + w), device_id_type=pl.DeviceIdType.MESH,
        )

    def send_halo(n, kinds):
        for kind in kinds:
            @pl.when(present(*kind[:3]))
            def _():
                halo_copy(n, kind).start()

    def wait_halo(n, kinds, recv):
        for kind in kinds:
            s, h, w, _part = kind

            @pl.when(present(-s, -h, -w) if recv else present(s, h, w))
            def _():
                if recv:
                    halo_copy(n, kind).wait_recv()
                else:
                    halo_copy(n, kind).wait_send()

    def stat_copy(n, d):
        return pltpu.make_async_remote_copy(
            src_ref=mine.at[n], dst_ref=theirs.at[n, d - 1],
            send_sem=stat_send.at[n], recv_sem=stat_recv.at[n],
            device_id=peer(d), device_id_type=pl.DeviceIdType.MESH,
        )

    lane = lax.broadcasted_iota(jnp.int32, (1, C), 1)
    even = lax.rem(lane, 2) == 0

    def send_stats(n, total, squares):
        total = group_sum(jnp.sum(total, axis=0, keepdims=True), C // GROUPS)
        squares = group_sum(jnp.sum(squares, axis=0, keepdims=True), C // GROUPS)
        mine[n] = jnp.where(even, total, squares)

        def start(d, c):
            stat_copy(n, d).start()
            return c

        lax.fori_loop(1, ndev, start, 0)

    def all_stats(n, of):
        return pltpu.make_async_copy(theirs.at[n], theirs.at[n], of.at[n])

    def get_affine(n, gain, shift):
        all_stats(n, stat_recv).wait()
        both = jnp.sum(theirs[n], axis=0) + mine[n]
        total = jnp.where(even, both, pltpu.roll(both, 1, 1))
        squares = jnp.where(even, pltpu.roll(both, C - 1, 1), both)
        count = T * area * (C // GROUPS) * ndev
        mean = total / count
        var = squares / count - mean * mean
        scale = gain[...] / jnp.sqrt(var + 1e-06)
        return 0.5 * scale, 0.5 * (shift[...] - mean * scale)

    def fold(v):
        return jnp.sum(v.reshape(-1, 8, C), axis=0)

    load.wait()

    def first(t, carry):
        v = feat[t].astype(jnp.float32).reshape(area, C)
        hid[pl.ds(t * area, area), :] = v
        return carry[0] + fold(v), carry[1] + fold(v * v)

    zero = jnp.zeros((8, C), jnp.float32)
    sums = lax.fori_loop(0, T, first, (zero, zero))

    def take_edges(n, start, count):
        for side, j in ((0, 0), (1, W - 1)):
            edge = hid[pl.ds(start * area + j, count * H, stride=W), :]
            cols[n, side, start : start + count] = edge.astype(jnp.bfloat16).reshape(count, H, C)
            for t in range(start, start + count):
                for hside, i in ((0, 0), (1, H - 1)):
                    at = t * area + i * W + j
                    pixel = jnp.broadcast_to(hid[at : at + 1, :], (2, C))
                    corners[n, hside, side, t] = pixel.astype(jnp.bfloat16)

    take_edges(0, 0, T)
    pl.semaphore_wait(barrier, ndev - 1)
    send_stats(0, *sums)
    send_halo(0, NEAR)
    send_halo(0, EARLY)
    send_halo(0, LATE)

    def fill_edges(n, act, lo, hi):
        def edges(t, c):
            known = jnp.logical_or(sec > 0, t >= 2)
            for hs, h in ((0, -1), (1, 1)):
                okh = jnp.logical_and(known, present(0, h, 0))
                i = 0 if hs == 0 else H + 1
                a = act(rows_in[n, hs, t].astype(jnp.float32))
                padded[t, i, LEAD : LEAD + W] = jnp.where(okh, a, 0.0)
                for ws, w in ((0, -1), (1, 1)):
                    okc = jnp.logical_and(okh, present(0, 0, w))
                    j = LEAD - 1 if ws == 0 else LEAD + W
                    a = act(corners_in[n, hs, ws, t].astype(jnp.float32))
                    padded[t, i, j : j + 1] = jnp.where(okc, a[0:1], 0.0)
            for ws, w in ((0, -1), (1, 1)):
                okw = jnp.logical_and(known, present(0, 0, w))
                j = LEAD - 1 if ws == 0 else LEAD + W
                a = jnp.where(okw, act(cols_in[n, ws, t].astype(jnp.float32)), 0.0)
                flat[pl.ds((t * (H + 2) + 1) * PW + j, H, stride=PW), :] = a
            for d in range(3):
                v = padded[t, :, LEAD - 1 + d : LEAD - 1 + d + W]
                cells[t, :, :, d * C : (d + 1) * C] = v.astype(jnp.bfloat16)
            return c

        lax.fori_loop(lo, hi, edges, 0)

    def own_frames(n, gain, shift):
        scale, bias = get_affine(n, gain, shift)

        def act(v):
            h = v * scale + bias
            return h * jnp.tanh(h) + h

        def inner(t, c):
            a = act(hid[pl.ds(t * area, area), :])
            padded[t + 2, 1 : H + 1, LEAD : LEAD + W] = a.reshape(H, W, C)
            return c

        lax.fori_loop(0, T, inner, 0)
        wait_halo(n, NEAR, True)
        fill_edges(n, act, 2, T + 2)
        return act

    def halo_frames(n, act):
        wait_halo(n, EARLY + LATE, True)

        def before(t, c):
            a = act(frames_in[n, t].astype(jnp.float32).reshape(area, C))
            a = jnp.where(sec > 0, a, 0.0)
            padded[t, 1 : H + 1, LEAD : LEAD + W] = a.reshape(H, W, C)
            return c

        lax.fori_loop(0, 2, before, 0)
        fill_edges(n, act, 0, 2)

    pairs = T // 2
    half = 18 * C

    def window(pair, q):
        return [cells[2 * pair + q, di : di + H].reshape(area, 3 * C) for di in range(3)]

    def conv_later(w):
        rows = [
            jnp.concatenate(window(pair, 2) + window(pair, 3), axis=-1) for pair in range(pairs)
        ]
        acc[...] = jnp.dot(
            jnp.concatenate(rows, axis=0), w[half : 2 * half], preferred_element_type=jnp.float32
        )

    def conv_pair(pair, w):
        lhs = jnp.concatenate(window(pair, 0) + window(pair, 1), axis=-1)
        part = jnp.dot(lhs, w[0:half], preferred_element_type=jnp.float32)
        return acc[pair * area : (pair + 1) * area, :] + part

    act = own_frames(0, gain1, shift1)
    weight_loads[0].wait()
    weight_loads[1].wait()
    total = squares = zero
    conv_later(w1)
    for pair in reversed(range(pairs)):
        if pair == 0:
            halo_frames(0, act)
        both = conv_pair(pair, w1)
        for f in range(2):
            v = both[:, f * C : (f + 1) * C]
            t = 2 * pair + f
            hid[t * area : (t + 1) * area, :] = v
            raw[t] = v.astype(jnp.bfloat16).reshape(H, W, C)
            total = total + fold(v)
            squares = squares + fold(v * v)
        take_edges(1, 2 * pair, 2)
        if pair == pairs - 1:
            send_halo(1, EARLY)
    send_stats(1, total, squares)
    send_halo(1, NEAR)
    send_halo(1, LATE)
    act = own_frames(1, gain2, shift2)
    weight_loads[2].wait()
    weight_loads[3].wait()
    conv_later(w2)
    stores = []
    for pair in reversed(range(pairs)):
        if pair == 0:
            halo_frames(1, act)
        both = conv_pair(pair, w2)
        for f in range(2):
            t = 2 * pair + f
            v = both[:, f * C : (f + 1) * C].reshape(H, W, C)
            result[t] = (feat[t].astype(jnp.float32) + v).astype(jnp.bfloat16)
        store = pltpu.make_async_copy(
            result.at[pl.ds(2 * pair, 2)], out_hbm.at[pl.ds(2 * pair, 2)], out_sem.at[pair]
        )
        store.start()
        stores.append(store)
    for n in range(2):
        wait_halo(n, SENDS, False)
        all_stats(n, stat_send).wait()
    for store in stores:
        store.wait()


def shards(sizes, features, gain1, shift1, k1, gain2, shift2, k2):
    T, H, W, C = features.shape
    ndev = sizes[0] * sizes[1] * sizes[2]
    bf, f32 = jnp.bfloat16, jnp.float32
    any_spec = pl.BlockSpec(memory_space=pl.ANY)
    vmem = pl.BlockSpec(memory_space=pltpu.VMEM)
    flat = lambda k: k.reshape(-1, k.shape[-1])
    row = lambda v: v.reshape(1, C)
    return pl.pallas_call(
        functools.partial(body, sizes),
        out_shape=jax.ShapeDtypeStruct(features.shape, bf),
        in_specs=[any_spec, vmem, vmem, any_spec, vmem, vmem, any_spec],
        out_specs=any_spec,
        scratch_shapes=[
            pltpu.VMEM((T, H, W, C), bf),
            pltpu.VMEM((T, H, W, C), bf),
            pltpu.VMEM((T, H, W, C), bf),
            pltpu.VMEM((T * H * W, C), f32),
            pltpu.VMEM((T + 2, H + 2, W + 2 * LEAD, C), f32),
            pltpu.VMEM((T + 2, H + 2, W, 3 * C), bf),
            pltpu.VMEM((T // 2 * H * W, 2 * C), f32),
            pltpu.VMEM((4 * 9 * C, 2 * C), bf),
            pltpu.VMEM((4 * 9 * C, 2 * C), bf),
            pltpu.VMEM((2, 2, T, H, C), bf),
            pltpu.VMEM((2, 2, 2, T, 2, C), bf),
            pltpu.VMEM((2, 2, H, W, C), bf),
            pltpu.VMEM((2, 2, T + 2, W, C), bf),
            pltpu.VMEM((2, 2, T + 2, H, C), bf),
            pltpu.VMEM((2, 2, 2, T + 2, 2, C), bf),
            pltpu.VMEM((2, 1, C), f32),
            pltpu.VMEM((2, ndev - 1, 1, C), f32),
            pltpu.SemaphoreType.DMA((5,)),
            pltpu.SemaphoreType.DMA((T // 2,)),
            pltpu.SemaphoreType.DMA((2,)),
            pltpu.SemaphoreType.DMA((2,)),
            pltpu.SemaphoreType.DMA((2, len(SENDS))),
            pltpu.SemaphoreType.DMA((2, len(SENDS))),
        ],
        compiler_params=pltpu.CompilerParams(
            collective_id=0, has_side_effects=True, vmem_limit_bytes=60 << 20
        ),
    )(features, row(gain1), row(shift1), flat(k1), row(gain2), row(shift2), flat(k2))


def solution(mesh):
    sizes = tuple(mesh.shape[a] for a in AXES)
    placed = (P("section", "th", "tw", None), P(), P(), P(), P(), P(), P())
    return jax.shard_map(
        functools.partial(shards, sizes),
        mesh=mesh,
        in_specs=placed,
        out_specs=P("section", "th", "tw", None),
        check_vma=False,
    )
```

```python
import functools

import jax
import jax.numpy as jnp
from jax import lax
from jax.experimental import pallas as pl
from jax.experimental.pallas import tpu as pltpu
from jax.sharding import PartitionSpec as P

GROUPS = 32
LEAD = 8
AXES = ("section", "th", "tw")
NEAR = [(0, h, w, 0) for h in (0, -1, 1) for w in (0, -1, 1) if (h, w) != (0, 0)]
EARLY = [(1, 0, 0, 0)]
LATE = [(1, 0, 0, 1)] + [(1, h, w, 0) for h in (0, -1, 1) for w in (0, -1, 1) if (h, w) != (0, 0)]
SENDS = NEAR + EARLY + LATE


def group_sum(row, per_group):
    lane = lax.broadcasted_iota(jnp.int32, row.shape, 1)
    chans = row.shape[1]
    step = 1
    while step < per_group:
        upper = lax.rem(lax.div(lane, step), 2) == 1
        row = row + jnp.where(upper, pltpu.roll(row, step, 1), pltpu.roll(row, chans - step, 1))
        step *= 2
    return row


def body(
    sizes, feat_hbm, gain1, shift1, k1_hbm, gain2, shift2, k2_hbm, out,
    feat, raw, hid, padded, cells, acc, w1, w2, cols, corners, frames_in, rows_in, cols_in, corners_in,
    mine, theirs, load_sem, stat_send, stat_recv, halo_send, halo_recv,
):
    ns, nh, nw = sizes
    ndev = ns * nh * nw
    T, H, W, C = feat.shape
    PW = padded.shape[2]
    area = H * W
    flat = padded.reshape(padded.shape[0] * padded.shape[1] * PW, C)
    sec, th, tw = (lax.axis_index(a) for a in AXES)
    rank = (sec * nh + th) * nw + tw
    taps = k1_hbm.shape[0]
    third = taps // 3

    load = pltpu.make_async_copy(feat_hbm, feat, load_sem.at[0])
    load.start()
    weight_loads = []
    for n, (src, dst) in enumerate(((k1_hbm, w1), (k2_hbm, w2))):
        for half in range(2):
            weight_loads.append(
                pltpu.make_async_copy(
                    src,
                    dst.at[pl.ds(half * third, taps), pl.ds(half * C, C)],
                    load_sem.at[1 + 2 * n + half],
                )
            )

    def peer(d):
        other = lax.rem(rank + d, ndev)
        return (lax.div(other, nh * nw), lax.rem(lax.div(other, nw), nh), lax.rem(other, nw))

    barrier = pltpu.get_barrier_semaphore()

    def greet(d, c):
        pl.semaphore_signal(barrier, inc=1, device_id=peer(d), device_id_type=pl.DeviceIdType.MESH)
        return c

    lax.fori_loop(1, ndev, greet, 0)
    for w in weight_loads:
        w.start()
    for w in (w1, w2):
        w[3 * third : 4 * third, 0:C] = jnp.zeros((third, C), jnp.bfloat16)
        w[0:third, C : 2 * C] = jnp.zeros((third, C), jnp.bfloat16)

    def present(s, h, w):
        ok = True
        for v, at, count in ((s, sec, ns), (h, th, nh), (w, tw, nw)):
            if v < 0:
                ok = jnp.logical_and(ok, at > 0)
            if v > 0:
                ok = jnp.logical_and(ok, at < count - 1)
        return ok

    chunk = H // 2

    def halo_copy(n, kind):
        s, h, w, part = kind
        k = SENDS.index(kind)
        frames = pl.ds(T - 2, 2) if s else pl.ds(0, T)
        into = pl.ds(0, 2) if s else pl.ds(2, T)
        source = feat if n == 0 else raw
        hs, ws = (0 if h > 0 else 1), (0 if w > 0 else 1)
        if h == 0 and w == 0:
            if part == 0:
                src, dst = source.at[T - 2, pl.ds(0, chunk)], frames_in.at[n, 0, pl.ds(0, chunk)]
            else:
                rest = pl.ds(chunk, 2 * H - chunk)
                src = source.at[pl.ds(T - 2, 2)].reshape(2 * H, W, C).at[rest]
                dst = frames_in.at[n].reshape(2 * H, W, C).at[rest]
        elif w == 0:
            src = source.at[frames, H - 1 if h > 0 else 0]
            dst = rows_in.at[n, hs, into]
        elif h == 0:
            src = cols.at[n, 1 if w > 0 else 0, frames]
            dst = cols_in.at[n, ws, into]
        else:
            src = corners.at[n, 1 if h > 0 else 0, 1 if w > 0 else 0, frames]
            dst = corners_in.at[n, hs, ws, into]
        return pltpu.make_async_remote_copy(
            src_ref=src, dst_ref=dst,
            send_sem=halo_send.at[n, k], recv_sem=halo_recv.at[n, k],
            device_id=(sec + s, th + h, tw + w), device_id_type=pl.DeviceIdType.MESH,
        )

    def send_halo(n, kinds):
        for kind in kinds:
            @pl.when(present(*kind[:3]))
            def _():
                halo_copy(n, kind).start()

    def wait_halo(n, kinds, recv):
        for kind in kinds:
            s, h, w, _part = kind

            @pl.when(present(-s, -h, -w) if recv else present(s, h, w))
            def _():
                if recv:
                    halo_copy(n, kind).wait_recv()
                else:
                    halo_copy(n, kind).wait_send()

    lane = lax.broadcasted_iota(jnp.int32, (1, C), 1)
    even = lax.rem(lane, 2) == 0

    def stat_copy(n, d):
        return pltpu.make_async_remote_copy(
            src_ref=mine.at[n], dst_ref=theirs.at[n, d - 1],
            send_sem=stat_send.at[n], recv_sem=stat_recv.at[n],
            device_id=peer(d), device_id_type=pl.DeviceIdType.MESH,
        )

    def send_stats(n, total, squares):
        total = group_sum(jnp.sum(total, axis=0, keepdims=True), C // GROUPS)
        squares = group_sum(jnp.sum(squares, axis=0, keepdims=True), C // GROUPS)
        mine[n] = jnp.where(even, total, squares)

        def start(d, c):
            stat_copy(n, d).start()
            return c

        lax.fori_loop(1, ndev, start, 0)

    def all_stats(n, of):
        return pltpu.make_async_copy(theirs.at[n], theirs.at[n], of.at[n])

    def get_affine(n, gain, shift):
        all_stats(n, stat_recv).wait()
        both = jnp.sum(theirs[n], axis=0) + mine[n]
        total = jnp.where(even, both, pltpu.roll(both, 1, 1))
        squares = jnp.where(even, pltpu.roll(both, C - 1, 1), both)
        count = T * area * (C // GROUPS) * ndev
        mean = total / count
        var = squares / count - mean * mean
        scale = gain[...] / jnp.sqrt(var + 1e-06)
        return 0.5 * scale, 0.5 * (shift[...] - mean * scale)

    def fold(v):
        return jnp.sum(v.reshape(-1, 8, C), axis=0)

    load.wait()

    def first(t, carry):
        v = feat[t].astype(jnp.float32).reshape(area, C)
        hid[pl.ds(t * area, area), :] = v
        return carry[0] + fold(v), carry[1] + fold(v * v)

    zero = jnp.zeros((8, C), jnp.float32)
    sums = lax.fori_loop(0, T, first, (zero, zero))

    def take_edges(n, start, count):
        for side, j in ((0, 0), (1, W - 1)):
            edge = hid[pl.ds(start * area + j, count * H, stride=W), :]
            cols[n, side, start : start + count] = edge.astype(jnp.bfloat16).reshape(count, H, C)
            for t in range(start, start + count):
                for hside, i in ((0, 0), (1, H - 1)):
                    at = t * area + i * W + j
                    pixel = jnp.broadcast_to(hid[at : at + 1, :], (2, C))
                    corners[n, hside, side, t] = pixel.astype(jnp.bfloat16)

    take_edges(0, 0, T)
    pl.semaphore_wait(barrier, ndev - 1)
    send_stats(0, *sums)
    send_halo(0, NEAR)
    send_halo(0, EARLY)
    send_halo(0, LATE)

    def fill_edges(n, act, lo, hi):
        def edges(t, c):
            known = jnp.logical_or(sec > 0, t >= 2)
            for hs, h in ((0, -1), (1, 1)):
                okh = jnp.logical_and(known, present(0, h, 0))
                i = 0 if hs == 0 else H + 1
                a = act(rows_in[n, hs, t].astype(jnp.float32))
                padded[t, i, LEAD : LEAD + W] = jnp.where(okh, a, 0.0)
                for ws, w in ((0, -1), (1, 1)):
                    okc = jnp.logical_and(okh, present(0, 0, w))
                    j = LEAD - 1 if ws == 0 else LEAD + W
                    a = act(corners_in[n, hs, ws, t].astype(jnp.float32))
                    padded[t, i, j : j + 1] = jnp.where(okc, a[0:1], 0.0)
            for ws, w in ((0, -1), (1, 1)):
                okw = jnp.logical_and(known, present(0, 0, w))
                j = LEAD - 1 if ws == 0 else LEAD + W
                a = jnp.where(okw, act(cols_in[n, ws, t].astype(jnp.float32)), 0.0)
                flat[pl.ds((t * (H + 2) + 1) * PW + j, H, stride=PW), :] = a
            for d in range(3):
                v = padded[t, :, LEAD - 1 + d : LEAD - 1 + d + W]
                cells[t, :, :, d * C : (d + 1) * C] = v.astype(jnp.bfloat16)
            return c

        lax.fori_loop(lo, hi, edges, 0)

    def own_frames(n, gain, shift):
        scale, bias = get_affine(n, gain, shift)

        def act(v):
            h = v * scale + bias
            return h * jnp.tanh(h) + h

        def inner(t, c):
            a = act(hid[pl.ds(t * area, area), :])
            padded[t + 2, 1 : H + 1, LEAD : LEAD + W] = a.reshape(H, W, C)
            return c

        lax.fori_loop(0, T, inner, 0)
        wait_halo(n, NEAR, True)
        fill_edges(n, act, 2, T + 2)
        return act

    def halo_frames(n, act):
        wait_halo(n, EARLY + LATE, True)

        def before(t, c):
            a = act(frames_in[n, t].astype(jnp.float32).reshape(area, C))
            a = jnp.where(sec > 0, a, 0.0)
            padded[t, 1 : H + 1, LEAD : LEAD + W] = a.reshape(H, W, C)
            return c

        lax.fori_loop(0, 2, before, 0)
        fill_edges(n, act, 0, 2)

    pairs = T // 2
    early = 20 * C

    def window(pair, q, di, lo=0, hi=3):
        return cells[2 * pair + q, di : di + H, :, lo * C : hi * C].reshape(area, (hi - lo) * C)

    def stacked(some, *where):
        return jnp.concatenate([window(pair, *where) for pair in some], axis=0)

    def conv_later(w):
        some = range(pairs)
        parts = [stacked(some, 2, 0, 2, 3), stacked(some, 2, 1), stacked(some, 2, 2)]
        parts += [stacked(some, 3, di) for di in range(3)]
        lhs = jnp.concatenate(parts, axis=-1)
        acc[...] = jnp.dot(lhs, w[early:], preferred_element_type=jnp.float32)

    def conv_first(some, w):
        parts = [stacked(some, q, di) for q in range(2) for di in range(3)]
        lhs = jnp.concatenate(parts + [stacked(some, 2, 0, 0, 2)], axis=-1)
        part = jnp.dot(lhs, w[0:early], preferred_element_type=jnp.float32)
        return acc[some[0] * area : (some[-1] + 1) * area, :] + part

    act = own_frames(0, gain1, shift1)
    weight_loads[0].wait()
    weight_loads[1].wait()
    total = squares = zero
    conv_later(w1)
    for pair in reversed(range(pairs)):
        if pair == 0:
            halo_frames(0, act)
        both = conv_first([pair], w1)
        for f in range(2):
            v = both[:, f * C : (f + 1) * C]
            t = 2 * pair + f
            hid[t * area : (t + 1) * area, :] = v
            raw[t] = v.astype(jnp.bfloat16).reshape(H, W, C)
            total = total + fold(v)
            squares = squares + fold(v * v)
        take_edges(1, 2 * pair, 2)
        if pair == pairs - 1:
            send_halo(1, EARLY)
    send_stats(1, total, squares)
    send_halo(1, NEAR)
    send_halo(1, LATE)
    act = own_frames(1, gain2, shift2)
    weight_loads[2].wait()
    weight_loads[3].wait()
    conv_later(w2)
    for pair in reversed(range(pairs)):
        if pair == 0:
            halo_frames(1, act)
        both = conv_first([pair], w2)
        for f in range(2):
            t = 2 * pair + f
            v = both[:, f * C : (f + 1) * C].reshape(H, W, C)
            out[t] = (feat[t].astype(jnp.float32) + v).astype(jnp.bfloat16)
    for n in range(2):
        wait_halo(n, SENDS, False)
    for n in range(2):
        all_stats(n, stat_send).wait()


def shards(sizes, features, gain1, shift1, k1, gain2, shift2, k2):
    T, H, W, C = features.shape
    ndev = sizes[0] * sizes[1] * sizes[2]
    bf, f32 = jnp.bfloat16, jnp.float32
    any_spec = pl.BlockSpec(memory_space=pl.ANY)
    vmem = pl.BlockSpec(memory_space=pltpu.VMEM)
    flat = lambda k: k.reshape(-1, k.shape[-1])
    row = lambda v: v.reshape(1, C)
    return pl.pallas_call(
        functools.partial(body, sizes),
        out_shape=pltpu.VMEM(features.shape, bf),
        in_specs=[any_spec, vmem, vmem, any_spec, vmem, vmem, any_spec],
        out_specs=vmem,
        scratch_shapes=[
            pltpu.VMEM((T, H, W, C), bf),
            pltpu.VMEM((T, H, W, C), bf),
            pltpu.VMEM((T * H * W, C), f32),
            pltpu.VMEM((T + 2, H + 2, W + 2 * LEAD, C), f32),
            pltpu.VMEM((T + 2, H + 2, W, 3 * C), bf),
            pltpu.VMEM((T // 2 * H * W, 2 * C), f32),
            pltpu.VMEM((4 * 9 * C, 2 * C), bf),
            pltpu.VMEM((4 * 9 * C, 2 * C), bf),
            pltpu.VMEM((2, 2, T, H, C), bf),
            pltpu.VMEM((2, 2, 2, T, 2, C), bf),
            pltpu.VMEM((2, 2, H, W, C), bf),
            pltpu.VMEM((2, 2, T + 2, W, C), bf),
            pltpu.VMEM((2, 2, T + 2, H, C), bf),
            pltpu.VMEM((2, 2, 2, T + 2, 2, C), bf),
            pltpu.VMEM((2, 1, C), f32),
            pltpu.VMEM((2, ndev - 1, 1, C), f32),
            pltpu.SemaphoreType.DMA((5,)),
            pltpu.SemaphoreType.DMA((2,)),
            pltpu.SemaphoreType.DMA((2,)),
            pltpu.SemaphoreType.DMA((2, len(SENDS))),
            pltpu.SemaphoreType.DMA((2, len(SENDS))),
        ],
        compiler_params=pltpu.CompilerParams(
            collective_id=0, has_side_effects=True, vmem_limit_bytes=60 << 20
        ),
    )(features, row(gain1), row(shift1), flat(k1), row(gain2), row(shift2), flat(k2))


def solution(mesh):
    sizes = tuple(mesh.shape[a] for a in AXES)
    placed = (P("section", "th", "tw", None), P(), P(), P(), P(), P(), P())
    return jax.shard_map(
        functools.partial(shards, sizes),
        mesh=mesh,
        in_specs=placed,
        out_specs=P("section", "th", "tw", None),
        check_vma=False,
    )
```

```python
import functools

import jax
import jax.numpy as jnp
from jax import lax
from jax.experimental import pallas as pl
from jax.experimental.pallas import tpu as pltpu
from jax.sharding import PartitionSpec as P

GROUPS = 32
LEAD = 8
AXES = ("section", "th", "tw")
NEAR = [(0, h, w, 0) for h in (0, -1, 1) for w in (0, -1, 1) if (h, w) != (0, 0)]
EARLY = [(1, 0, 0, 0)]
LATE = [(1, 0, 0, 1)] + [(1, h, w, 0) for h in (0, -1, 1) for w in (0, -1, 1) if (h, w) != (0, 0)]
SENDS = NEAR + EARLY + LATE


def group_sum(row, per_group):
    lane = lax.broadcasted_iota(jnp.int32, row.shape, 1)
    chans = row.shape[1]
    step = 1
    while step < per_group:
        upper = lax.rem(lax.div(lane, step), 2) == 1
        row = row + jnp.where(upper, pltpu.roll(row, step, 1), pltpu.roll(row, chans - step, 1))
        step *= 2
    return row


def body(
    sizes, feat_hbm, gain1, shift1, k1_hbm, gain2, shift2, k2_hbm, out,
    feat, raw, hid, padded, cells, acc, w1, w2, cols, corners, frames_in, rows_in, cols_in, corners_in,
    mine, theirs, load_sem, stat_send, stat_recv, halo_send, halo_recv,
):
    ns, nh, nw = sizes
    ndev = ns * nh * nw
    T, H, W, C = feat.shape
    PW = padded.shape[2]
    area = H * W
    flat = padded.reshape(padded.shape[0] * padded.shape[1] * PW, C)
    sec, th, tw = (lax.axis_index(a) for a in AXES)
    rank = (sec * nh + th) * nw + tw
    taps = k1_hbm.shape[0]
    third = taps // 3

    load = pltpu.make_async_copy(feat_hbm, feat, load_sem.at[0])
    load.start()
    weight_loads = []
    for n, (src, dst) in enumerate(((k1_hbm, w1), (k2_hbm, w2))):
        for half in range(2):
            weight_loads.append(
                pltpu.make_async_copy(
                    src,
                    dst.at[pl.ds(half * third, taps), pl.ds(half * C, C)],
                    load_sem.at[1 + 2 * n + half],
                )
            )

    def peer(d):
        other = lax.rem(rank + d, ndev)
        return (lax.div(other, nh * nw), lax.rem(lax.div(other, nw), nh), lax.rem(other, nw))

    barrier = pltpu.get_barrier_semaphore()

    def greet(d, c):
        pl.semaphore_signal(barrier, inc=1, device_id=peer(d), device_id_type=pl.DeviceIdType.MESH)
        return c

    lax.fori_loop(1, ndev, greet, 0)
    for w in weight_loads:
        w.start()
    for w in (w1, w2):
        w[3 * third : 4 * third, 0:C] = jnp.zeros((third, C), jnp.bfloat16)
        w[0:third, C : 2 * C] = jnp.zeros((third, C), jnp.bfloat16)

    def present(s, h, w):
        ok = True
        for v, at, count in ((s, sec, ns), (h, th, nh), (w, tw, nw)):
            if v < 0:
                ok = jnp.logical_and(ok, at > 0)
            if v > 0:
                ok = jnp.logical_and(ok, at < count - 1)
        return ok

    chunk = H // 2

    def halo_copy(n, kind):
        s, h, w, part = kind
        k = SENDS.index(kind)
        frames = pl.ds(T - 2, 2) if s else pl.ds(0, T)
        into = pl.ds(0, 2) if s else pl.ds(2, T)
        source = feat if n == 0 else raw
        hs, ws = (0 if h > 0 else 1), (0 if w > 0 else 1)
        if h == 0 and w == 0:
            if part == 0:
                src, dst = source.at[T - 2, pl.ds(0, chunk)], frames_in.at[n, 0, pl.ds(0, chunk)]
            else:
                rest = pl.ds(chunk, 2 * H - chunk)
                src = source.at[pl.ds(T - 2, 2)].reshape(2 * H, W, C).at[rest]
                dst = frames_in.at[n].reshape(2 * H, W, C).at[rest]
        elif w == 0:
            src = source.at[frames, H - 1 if h > 0 else 0]
            dst = rows_in.at[n, hs, into]
        elif h == 0:
            src = cols.at[n, 1 if w > 0 else 0, frames]
            dst = cols_in.at[n, ws, into]
        else:
            src = corners.at[n, 1 if h > 0 else 0, 1 if w > 0 else 0, frames]
            dst = corners_in.at[n, hs, ws, into]
        return pltpu.make_async_remote_copy(
            src_ref=src, dst_ref=dst,
            send_sem=halo_send.at[n, k], recv_sem=halo_recv.at[n, k],
            device_id=(sec + s, th + h, tw + w), device_id_type=pl.DeviceIdType.MESH,
        )

    def send_halo(n, kinds):
        for kind in kinds:
            @pl.when(present(*kind[:3]))
            def _():
                halo_copy(n, kind).start()

    def wait_halo(n, kinds, recv):
        for kind in kinds:
            s, h, w, _part = kind

            @pl.when(present(-s, -h, -w) if recv else present(s, h, w))
            def _():
                if recv:
                    halo_copy(n, kind).wait_recv()
                else:
                    halo_copy(n, kind).wait_send()

    lane = lax.broadcasted_iota(jnp.int32, (1, C), 1)
    even = lax.rem(lane, 2) == 0

    def stat_copy(n, d):
        return pltpu.make_async_remote_copy(
            src_ref=mine.at[n], dst_ref=theirs.at[n, d - 1],
            send_sem=stat_send.at[n], recv_sem=stat_recv.at[n],
            device_id=peer(d), device_id_type=pl.DeviceIdType.MESH,
        )

    def send_stats(n, total, squares):
        total = group_sum(jnp.sum(total, axis=0, keepdims=True), C // GROUPS)
        squares = group_sum(jnp.sum(squares, axis=0, keepdims=True), C // GROUPS)
        mine[n] = jnp.where(even, total, squares)

        def start(d, c):
            stat_copy(n, d).start()
            return c

        lax.fori_loop(1, ndev, start, 0)

    def all_stats(n, of):
        return pltpu.make_async_copy(theirs.at[n], theirs.at[n], of.at[n])

    def get_affine(n, gain, shift):
        all_stats(n, stat_recv).wait()
        both = jnp.sum(theirs[n], axis=0) + mine[n]
        total = jnp.where(even, both, pltpu.roll(both, 1, 1))
        squares = jnp.where(even, pltpu.roll(both, C - 1, 1), both)
        count = T * area * (C // GROUPS) * ndev
        mean = total / count
        var = squares / count - mean * mean
        scale = gain[...] / jnp.sqrt(var + 1e-06)
        return 0.5 * scale, 0.5 * (shift[...] - mean * scale)

    def fold(v):
        return jnp.sum(v.reshape(-1, 8, C), axis=0)

    load.wait()

    def first(t, carry):
        v = feat[t].astype(jnp.float32).reshape(area, C)
        hid[pl.ds(t * area, area), :] = v
        return carry[0] + fold(v), carry[1] + fold(v * v)

    zero = jnp.zeros((8, C), jnp.float32)
    sums = lax.fori_loop(0, T, first, (zero, zero))

    def take_edges(n, start, count):
        for side, j in ((0, 0), (1, W - 1)):
            edge = hid[pl.ds(start * area + j, count * H, stride=W), :]
            cols[n, side, start : start + count] = edge.astype(jnp.bfloat16).reshape(count, H, C)
            for t in range(start, start + count):
                for hside, i in ((0, 0), (1, H - 1)):
                    at = t * area + i * W + j
                    pixel = jnp.broadcast_to(hid[at : at + 1, :], (2, C))
                    corners[n, hside, side, t] = pixel.astype(jnp.bfloat16)

    take_edges(0, 0, T)
    pl.semaphore_wait(barrier, ndev - 1)
    send_stats(0, *sums)
    send_halo(0, NEAR)
    send_halo(0, EARLY)
    send_halo(0, LATE)

    def fill_edges(n, act, lo, hi):
        def edges(t, c):
            known = jnp.logical_or(sec > 0, t >= 2)
            for hs, h in ((0, -1), (1, 1)):
                okh = jnp.logical_and(known, present(0, h, 0))
                i = 0 if hs == 0 else H + 1
                a = act(rows_in[n, hs, t].astype(jnp.float32))
                padded[t, i, LEAD : LEAD + W] = jnp.where(okh, a, 0.0)
                for ws, w in ((0, -1), (1, 1)):
                    okc = jnp.logical_and(okh, present(0, 0, w))
                    j = LEAD - 1 if ws == 0 else LEAD + W
                    a = act(corners_in[n, hs, ws, t].astype(jnp.float32))
                    padded[t, i, j : j + 1] = jnp.where(okc, a[0:1], 0.0)
            for ws, w in ((0, -1), (1, 1)):
                okw = jnp.logical_and(known, present(0, 0, w))
                j = LEAD - 1 if ws == 0 else LEAD + W
                a = jnp.where(okw, act(cols_in[n, ws, t].astype(jnp.float32)), 0.0)
                flat[pl.ds((t * (H + 2) + 1) * PW + j, H, stride=PW), :] = a
            for d in range(3):
                v = padded[t, :, LEAD - 1 + d : LEAD - 1 + d + W]
                cells[t, :, :, d * C : (d + 1) * C] = v.astype(jnp.bfloat16)
            return c

        lax.fori_loop(lo, hi, edges, 0)

    def own_frames(n, gain, shift):
        scale, bias = get_affine(n, gain, shift)

        def act(v):
            h = v * scale + bias
            return h * jnp.tanh(h) + h

        def inner(t, c):
            a = act(hid[pl.ds(t * area, area), :])
            padded[t + 2, 1 : H + 1, LEAD : LEAD + W] = a.reshape(H, W, C)
            return c

        lax.fori_loop(0, T, inner, 0)
        wait_halo(n, NEAR, True)
        fill_edges(n, act, 2, T + 2)
        return act

    def halo_frames(n, act):
        wait_halo(n, EARLY + LATE, True)

        def before(t, c):
            a = act(frames_in[n, t].astype(jnp.float32).reshape(area, C))
            a = jnp.where(sec > 0, a, 0.0)
            padded[t, 1 : H + 1, LEAD : LEAD + W] = a.reshape(H, W, C)
            return c

        lax.fori_loop(0, 2, before, 0)
        fill_edges(n, act, 0, 2)

    pairs = T // 2
    early = 20 * C

    def window(pair, q, di, lo=0, hi=3):
        return cells[2 * pair + q, di : di + H, :, lo * C : hi * C].reshape(area, (hi - lo) * C)

    def stacked(some, *where):
        return jnp.concatenate([window(pair, *where) for pair in some], axis=0)

    def conv_later(w):
        some = range(pairs)
        parts = [stacked(some, 2, 0, 2, 3), stacked(some, 2, 1), stacked(some, 2, 2)]
        parts += [stacked(some, 3, di) for di in range(3)]
        lhs = jnp.concatenate(parts, axis=-1)
        for m in range(pairs):
            acc[m * area : (m + 1) * area, :] = jnp.dot(lhs[m * area : (m + 1) * area], w[early:], preferred_element_type=jnp.float32)

    def conv_first(some, w):
        parts = [stacked(some, q, di) for q in range(2) for di in range(3)]
        lhs = jnp.concatenate(parts + [stacked(some, 2, 0, 0, 2)], axis=-1)
        part = jnp.dot(lhs, w[0:early], preferred_element_type=jnp.float32)
        return acc[some[0] * area : (some[-1] + 1) * area, :] + part

    act = own_frames(0, gain1, shift1)
    weight_loads[0].wait()
    weight_loads[1].wait()
    total = squares = zero
    conv_later(w1)
    for pair in reversed(range(pairs)):
        if pair == 0:
            halo_frames(0, act)
        both = conv_first([pair], w1)
        for f in range(2):
            v = both[:, f * C : (f + 1) * C]
            t = 2 * pair + f
            hid[t * area : (t + 1) * area, :] = v
            raw[t] = v.astype(jnp.bfloat16).reshape(H, W, C)
            total = total + fold(v)
            squares = squares + fold(v * v)
        take_edges(1, 2 * pair, 2)
        if pair == pairs - 1:
            send_halo(1, EARLY)
    send_stats(1, total, squares)
    send_halo(1, NEAR)
    send_halo(1, LATE)
    act = own_frames(1, gain2, shift2)
    weight_loads[2].wait()
    weight_loads[3].wait()
    conv_later(w2)
    for pair in reversed(range(pairs)):
        if pair == 0:
            halo_frames(1, act)
        both = conv_first([pair], w2)
        for f in range(2):
            t = 2 * pair + f
            v = both[:, f * C : (f + 1) * C].reshape(H, W, C)
            out[t] = (feat[t].astype(jnp.float32) + v).astype(jnp.bfloat16)
    for n in range(2):
        wait_halo(n, SENDS, False)
    for n in range(2):
        all_stats(n, stat_send).wait()


def shards(sizes, features, gain1, shift1, k1, gain2, shift2, k2):
    T, H, W, C = features.shape
    ndev = sizes[0] * sizes[1] * sizes[2]
    bf, f32 = jnp.bfloat16, jnp.float32
    any_spec = pl.BlockSpec(memory_space=pl.ANY)
    vmem = pl.BlockSpec(memory_space=pltpu.VMEM)
    flat = lambda k: k.reshape(-1, k.shape[-1])
    row = lambda v: v.reshape(1, C)
    return pl.pallas_call(
        functools.partial(body, sizes),
        out_shape=pltpu.VMEM(features.shape, bf),
        in_specs=[any_spec, vmem, vmem, any_spec, vmem, vmem, any_spec],
        out_specs=vmem,
        scratch_shapes=[
            pltpu.VMEM((T, H, W, C), bf),
            pltpu.VMEM((T, H, W, C), bf),
            pltpu.VMEM((T * H * W, C), f32),
            pltpu.VMEM((T + 2, H + 2, W + 2 * LEAD, C), f32),
            pltpu.VMEM((T + 2, H + 2, W, 3 * C), bf),
            pltpu.VMEM((T // 2 * H * W, 2 * C), f32),
            pltpu.VMEM((4 * 9 * C, 2 * C), bf),
            pltpu.VMEM((4 * 9 * C, 2 * C), bf),
            pltpu.VMEM((2, 2, T, H, C), bf),
            pltpu.VMEM((2, 2, 2, T, 2, C), bf),
            pltpu.VMEM((2, 2, H, W, C), bf),
            pltpu.VMEM((2, 2, T + 2, W, C), bf),
            pltpu.VMEM((2, 2, T + 2, H, C), bf),
            pltpu.VMEM((2, 2, 2, T + 2, 2, C), bf),
            pltpu.VMEM((2, 1, C), f32),
            pltpu.VMEM((2, ndev - 1, 1, C), f32),
            pltpu.SemaphoreType.DMA((5,)),
            pltpu.SemaphoreType.DMA((2,)),
            pltpu.SemaphoreType.DMA((2,)),
            pltpu.SemaphoreType.DMA((2, len(SENDS))),
            pltpu.SemaphoreType.DMA((2, len(SENDS))),
        ],
        compiler_params=pltpu.CompilerParams(
            collective_id=0, has_side_effects=True, vmem_limit_bytes=60 << 20
        ),
    )(features, row(gain1), row(shift1), flat(k1), row(gain2), row(shift2), flat(k2))


def solution(mesh):
    sizes = tuple(mesh.shape[a] for a in AXES)
    placed = (P("section", "th", "tw", None), P(), P(), P(), P(), P(), P())
    return jax.shard_map(
        functools.partial(shards, sizes),
        mesh=mesh,
        in_specs=placed,
        out_specs=P("section", "th", "tw", None),
        check_vma=False,
    )
```
